32 devices in a mesh: blk: 2 (over y), fsdp: 16 (over z, x, core).
Axes of the slice: x: 2, y: 2, z: 4, core: 2. Of those that a mesh axis runs over, the one named last changes fastest.
Arguments:
- tokens: bfloat16 [2, 2048, 2304], P('blk', 'fsdp'), may hold values from -6 to 6
- cotangent: bfloat16 [2, 2048, 512], P('blk', 'fsdp'), may hold values from -6 to 6
- weights: float32 [2, 2304, 512], P('blk', 'fsdp'), may hold values from -6 to 6
- moment_one: float32 [2, 2304, 512], P('blk', 'fsdp'), may hold values from -6 to 6
- moment_two: float32 [2, 2304, 512], P('blk', 'fsdp'), may hold values from 1 to 16
- gossip: int32 [2, 3], P('blk'), may hold values from 1 to 8
Outputs:
- key_out: bfloat16 [2, 2048, 512], P('blk', 'fsdp')
- input_grad: bfloat16 [2, 2048, 2304], P('blk', 'fsdp')
- weights_out: float32 [2, 2304, 512], P('blk', 'fsdp')
- moment_one_out: float32 [2, 2304, 512], P('blk', 'fsdp')
- moment_two_out: float32 [2, 2304, 512], P('blk', 'fsdp')
The draws below stay inside these ranges and needn't reach their ends.
Inputs may be any that keep to these rules, and one draw needn't show every extreme that they name: `gossip`: row r holds the weights given to replica r - 1, to replica r itself and to replica r + 1 on the closed cycle of 2 replicas.
All inputs are finite; a program needn't handle non-finite values.
Results may differ from the reference program's by a relative error of at most 0.005.
Values may be sent and summed in bfloat16 or wider, within the bound.
A program may use at most 64 MiB of HBM per device.

```python
import math
import jax
import jax.numpy as jnp
from jax import lax

DIN = 2304
HKD = 512
TOKENS = 2048
REPLICAS = 2


def touch_ends(result, stream_key, smallest, top_value):
    longest = result.shape.index(max(result.shape))
    spots = []
    for shift in (0, 1):
        where = [jax.random.randint(jax.random.fold_in(stream_key, axis), (), 0, length) for axis, length in enumerate(result.shape)]
        where[longest] = (where[longest] + shift) % result.shape[longest]
        spots.append(tuple(where))
    return result.at[spots[0]].set(smallest).at[spots[1]].set(top_value)


def raised(values, own_key, source, target, blocks, factor):
    def block_of(dim):
        return (jnp.arange(values.shape[dim]) // (values.shape[dim] // blocks)).reshape((-1,) + (1,) * (values.ndim - 1 - dim))

    one_side = jax.random.permutation(own_key, blocks)[block_of(target)]
    second = (block_of(target) + blocks // 2) % blocks
    return jnp.where((block_of(source) == one_side) | (block_of(source) == second), factor * values, values)


def levels(stream_key, extent, cuts, smallest, high):
    loudness, own = 1.0, jax.random.fold_in(stream_key, 6)
    for dim, blocks in cuts:
        heights = jnp.exp(jax.random.uniform(jax.random.fold_in(own, dim), (blocks,), jnp.float32, smallest / len(cuts), high / len(cuts)))
        loudness = loudness * jnp.repeat(heights, extent[dim] // blocks).reshape([-1 if axis == dim else 1 for axis in range(len(extent))])
    return loudness


def scatter_about(rng, extent, scale, most, split=(), dtype=jnp.bfloat16):
    values = scale * jax.random.normal(rng, extent, jnp.float32)
    if split:
        values = values * levels(rng, extent, split, -0.22, 0.18)
    return jnp.clip(values, -most, most).astype(dtype)


def bell_draw_with(key, shape, spread, most, shards, heavy, held_as=jnp.bfloat16):
    drawn = spread * jax.random.normal(key, shape, jnp.float32)
    if shards:
        drawn = drawn * levels(key, shape, shards, -0.22, 0.18)
    return jnp.clip(raised(drawn, jax.random.fold_in(key, 3), *heavy), -most, most).astype(held_as)


def setup_inputs(seed: int = 0) -> dict:
    keys = jax.random.split(jax.random.key(seed), 7)
    tokens = bell_draw_with(keys[0], (REPLICAS, TOKENS, DIN), 1.0, 6.0, ((0, 2), (1, 16)), (1, 2, 16, 2.0))
    cotangent = scatter_about(keys[1], (REPLICAS, TOKENS, HKD), 1.0, 6.0, ((0, 2), (1, 16)))
    weights = scatter_about(keys[2], (REPLICAS, DIN, HKD), 1.0, 6.0, ((0, 2), (1, 16)), jnp.float32)
    moment_one = scatter_about(keys[3], (REPLICAS, DIN, HKD), 1.0, 6.0, ((0, 2), (1, 16)), jnp.float32)
    moment_two = jnp.clip(jnp.exp(math.log(16.0) - 2.7725887 * jax.random.uniform(keys[4], (REPLICAS, DIN, HKD), jnp.float32) ** levels(keys[4], (REPLICAS, DIN, HKD), ((0, 2), (1, 16)), -0.2, 0.2)), 1.0, 16.0)
    gossip = touch_ends(jax.random.randint(keys[5], (REPLICAS, 3), 1, 9), jax.random.fold_in(keys[5], 1), 1, 8).astype(jnp.int32)
    return {"tokens": tokens, "cotangent": cotangent, "weights": weights, "moment_one": moment_one, "moment_two": moment_two, "gossip": gossip}


beta_one = 0.9
beta_two = 0.95
learn_rate = 0.05
weight_decay = 0.1
epsilon = 1e-08
correct_one = 1.0 - beta_one ** 5
correct_two = 1.0 - beta_two ** 5

def replica_step(inputs):
    activations, upstream, weights, moment_one, moment_two = inputs
    factor = 1.0 / math.sqrt(DIN)
    compute_weights = weights.astype(jnp.bfloat16)
    key_out = (jnp.dot(activations, compute_weights, preferred_element_type=jnp.float32) * factor).astype(jnp.bfloat16)
    input_grad = (jnp.dot(upstream, compute_weights.T, preferred_element_type=jnp.float32) * factor).astype(jnp.bfloat16)
    gradient = jnp.dot(activations.T, upstream, preferred_element_type=jnp.float32) * factor
    moment_one_out = beta_one * moment_one + (1.0 - beta_one) * gradient
    moment_two_out = beta_two * moment_two + (1.0 - beta_two) * gradient * gradient
    update = moment_one_out / correct_one / (jnp.sqrt(moment_two_out / correct_two) + epsilon)
    stepped = weights - learn_rate * (update + weight_decay * weights)
    return (key_out, input_grad, stepped, moment_one_out, moment_two_out)

def reference(tokens, cotangent, weights, moment_one, moment_two, gossip):
    key_out, input_grad, stepped, moment_one_out, moment_two_out = lax.map(replica_step, (tokens, cotangent, weights, moment_one, moment_two))
    left_side = jnp.roll(stepped, 1, axis=0)
    right_side = jnp.roll(stepped, -1, axis=0)
    mix_weights = gossip.astype(jnp.float32)
    weight_left = mix_weights[:, 0][:, None, None]
    weight_self = mix_weights[:, 1][:, None, None]
    weight_right = mix_weights[:, 2][:, None, None]
    weights_out = (weight_left * left_side + weight_self * stepped + weight_right * right_side) / (weight_left + weight_self + weight_right)
    return (key_out, input_grad, weights_out, moment_one_out, moment_two_out)
```

```python
import functools
import math

import jax
import jax.numpy as jnp
from jax import lax
from jax.experimental import pallas as pl
from jax.experimental.pallas import tpu as pltpu
from jax.sharding import PartitionSpec as P

beta_one = 0.9
beta_two = 0.95
learn_rate = 0.05
weight_decay = 0.1
epsilon = 1e-08
correct_one = 1.0 - beta_one**5
correct_two = 1.0 - beta_two**5

BF = jnp.bfloat16
F32 = jnp.float32


def kernel(
    nz, nb, cut, factor,
    tok_h, cot_h, w_h, m1_h, m2_h, gos,
    key_o, ig_o, avg_o, m1_o, m2_o,
    w_v, m1_v, m2_v, tok2, cot2, wfull, part,
    xs_a, xr_a, zs_a, zr_a, zs_b, zr_b, xs_b, xr_b, ss, sr,
    load_sem, ce_s, ce_r, az_s, az_r, ax_s, ax_r, bx_s, bx_r, bz_s, bz_r,
    ca_s, ca_r, cb_s, cb_r, rax_s, rax_r, rza_s, rza_r, rzb_s, rzb_r, rbx_s, rbx_r, y_s, y_r,
):
    T, D = tok_h.shape
    R, H = w_h.shape
    me = lax.axis_index("fsdp")
    rep = lax.axis_index("blk")
    z = me // 4
    x = (me // 2) % 2
    c = me % 2
    low, high = cut, R - cut

    def dev(zz, xx, cc):
        return (rep, zz * 4 + xx * 2 + cc)

    def remote(src, dst, s, r, device):
        return pltpu.make_async_remote_copy(
            src_ref=src, dst_ref=dst, send_sem=s, recv_sem=r,
            device_id=device, device_id_type=pl.DeviceIdType.MESH,
        )

    loads = [
        pltpu.make_async_copy(w_h, w_v, load_sem.at[0]),
        pltpu.make_async_copy(cot_h, cot2.at[0:T], load_sem.at[1]),
        pltpu.make_async_copy(tok_h, tok2.at[0:T], load_sem.at[2]),
        pltpu.make_async_copy(m1_h, m1_v, load_sem.at[3]),
        pltpu.make_async_copy(m2_h, m2_v, load_sem.at[4]),
    ]
    for load in loads:
        load.start()

    barrier = pltpu.get_barrier_semaphore()

    def greet(device):
        pl.semaphore_signal(barrier, inc=1, device_id=device, device_id_type=pl.DeviceIdType.MESH)

    after = lax.rem(rep + 1, nb)
    before = lax.rem(rep + nb - 1, nb)
    x_dev = dev(z, 1 - x, c)
    c_dev = dev(z, x, 1 - c)
    greet(x_dev)
    greet(c_dev)
    greet((after, me))
    if nb > 2:
        greet((before, me))

    @pl.when(z > 0)
    def _():
        greet(dev(z - 1, x, c))

    @pl.when(z < nz - 1)
    def _():
        greet(dev(z + 1, x, c))

    loads[0].wait()
    wfull[z, x, c] = w_v[...].astype(BF)
    pl.semaphore_wait(barrier, (3 if nb > 2 else 2) + jnp.minimum(z, 1) + jnp.minimum(nz - 1 - z, 1) + (1 if nb > 1 else 0))

    ex_c = remote(cot_h, cot2.at[T : 2 * T], ce_s.at[0], ce_r.at[0], c_dev)
    ex_t = remote(tok_h, tok2.at[T : 2 * T], ce_s.at[1], ce_r.at[1], c_dev)
    ex_c.start()
    ex_t.start()

    def a_z(d, zz):
        ref = wfull.at[zz, x, c, 0:low]
        return remote(ref, ref, az_s.at[d, zz], az_r.at[zz], dev(z + 1 - 2 * d, x, c))

    def a_x(zz):
        ref = wfull.at[zz, x, c, 0:low]
        return remote(ref, ref, ax_s.at[zz], ax_r.at[zz], x_dev)

    def a_x_in(zz):
        ref = wfull.at[zz, 1 - x, c, 0:low]
        return remote(ref, ref, ax_s.at[zz], ax_r.at[zz], x_dev)

    own_b = wfull.at[z, x, c, low:R]
    b_x = remote(own_b, own_b, bx_s, bx_r, x_dev)

    def b_z(d, zz):
        ref = wfull.at[zz, :, c, low:R]
        return remote(ref, ref, bz_s.at[d, zz], bz_r.at[zz], dev(z + 1 - 2 * d, x, c))

    def core_a(zz, cc):
        ref = wfull.at[zz, :, cc, 0:low]
        return remote(ref, ref, ca_s.at[zz], ca_r.at[zz], c_dev)

    def core_b(zz, cc):
        ref = wfull.at[zz, :, cc, low:R]
        return remote(ref, ref, cb_s.at[zz], cb_r.at[zz], c_dev)

    b_x.start()

    @pl.when(z < nz - 1)
    def _():
        a_z(0, z).start()

    @pl.when(z > 0)
    def _():
        a_z(1, z).start()

    a_x(z).start()

    def gather_pair():
        b_x.wait_recv()

        @pl.when(z < nz - 1)
        def _():
            b_z(0, z).start()

        @pl.when(z > 0)
        def _():
            b_z(1, z).start()

        core_b(z, c).start()

    def gather_hop(k):
        for d in (0, 1):
            zz = z - k if d == 0 else z + k

            @pl.when((zz >= 0) & (zz < nz))
            def _():
                further = (z < nz - 1) if d == 0 else (z > 0)
                a_z(d, zz).wait_recv()

                @pl.when(further)
                def _():
                    a_z(d, zz).start()

                a_x(zz).start()
                b_z(d, zz).wait_recv()

                @pl.when(further)
                def _():
                    b_z(d, zz).start()

                core_b(zz, c).start()

    gather_pair()

    loads[1].wait()
    loads[2].wait()
    ex_c.wait_recv()
    ex_t.wait_recv()
    wide = math.gcd(D, 384)

    def partial(j, carry):
        at = pl.multiple_of(j * wide, wide)
        part[pl.ds(at, wide), :] = lax.dot_general(
            tok2[:, pl.ds(at, wide)], cot2[...], (((0,), (0,)), ((), ())), preferred_element_type=F32
        )
        return carry

    lax.fori_loop(0, D // wide, partial, 0)

    def mine(zz, xx, start, size):
        at = pl.multiple_of((zz * 4 + xx * 2 + c) * R + start, 16)
        return part[pl.ds(at, size), :]

    up_first = jnp.where(z >= nz // 2, 1, 0)

    def red_x(zz):
        return remote(xs_a.at[zz], xr_a.at[zz], rax_s.at[zz], rax_r.at[zz], x_dev)

    def send_a(k, carry):
        zz = (1 - up_first) * (nz - 1 - k) + up_first * k
        xs_a[zz] = mine(zz, 1 - x, 0, low).astype(BF)
        red_x(zz).start()
        return carry

    lax.fori_loop(0, nz, send_a, 0)

    def red_za(d, zz):
        return remote(zs_a.at[d, zz], zr_a.at[d, zz], rza_s.at[d, zz], rza_r.at[d, zz], dev(z + 1 - 2 * d, x, c))

    def red_zb(d, zz):
        return remote(zs_b.at[d, zz], zr_b.at[d, zz], rzb_s.at[d, zz], rzb_r.at[d, zz], dev(z + 1 - 2 * d, x, c))

    def chain(d, body):
        count = (1 - d) * (nz - 1 - z) + d * z
        fed = (1 - d) * z + d * (nz - 1 - z) > 0

        def step(k, carry):
            body((1 - d) * (nz - 1 - k) + d * k, fed)
            return carry

        lax.fori_loop(0, count, step, 0)

    def chain_a(d):
        def body(zz, fed):
            red_x(zz).wait_recv()
            base = mine(zz, x, 0, low) + xr_a[zz].astype(F32)

            @pl.when(fed)
            def _():
                red_za(d, zz).wait_recv()
                zs_a[d, zz] = (base + zr_a[d, zz].astype(F32)).astype(BF)

            @pl.when(jnp.logical_not(fed))
            def _():
                zs_a[d, zz] = base.astype(BF)

            red_za(d, zz).start()

        chain(d, body)

    def chain_b(d):
        def body(zz, fed):
            @pl.when(fed)
            def _():
                red_zb(d, zz).wait_recv()
                for xx in (0, 1):
                    zs_b[d, zz, xx] = (mine(zz, xx, low, high) + zr_b[d, zz, xx].astype(F32)).astype(BF)

            @pl.when(jnp.logical_not(fed))
            def _():
                for xx in (0, 1):
                    zs_b[d, zz, xx] = mine(zz, xx, low, high).astype(BF)

            red_zb(d, zz).start()

        chain(d, body)

    gather_hop(1)
    chain_b(up_first)
    if nz > 2:
        gather_hop(2)
    chain_b(1 - up_first)
    chain_a(up_first)
    for k in range(3, nz):
        gather_hop(k)
    chain_a(1 - up_first)

    def own_at(xx, start):
        return pl.ds(pl.multiple_of((z * 4 + xx * 2 + c) * R + start, 16), low if start == 0 else high)

    for d in (0, 1):
        @pl.when((z > 0) if d == 0 else (z < nz - 1))
        def _():
            red_zb(d, z).wait_recv()
            for xx in (0, 1):
                part[own_at(xx, low), :] += zr_b[d, z, xx].astype(F32)

    red_bx = remote(xs_b, xr_b, rbx_s, rbx_r, x_dev)
    xs_b[...] = mine(z, 1 - x, low, high).astype(BF)
    red_bx.start()
    red_x(z).wait_recv()
    part[own_at(x, 0), :] += xr_a[z].astype(F32)
    for d in (0, 1):
        @pl.when((z > 0) if d == 0 else (z < nz - 1))
        def _():
            red_za(d, z).wait_recv()
            part[own_at(x, 0), :] += zr_a[d, z].astype(F32)

    loads[3].wait()
    loads[4].wait()
    red_bx.wait_recv()
    part[own_at(x, low), :] += xr_b[...].astype(F32)

    gradient = part[pl.ds(pl.multiple_of(me * R, 16), R), :] * factor
    new_one = beta_one * m1_v[...] + (1.0 - beta_one) * gradient
    new_two = beta_two * m2_v[...] + (1.0 - beta_two) * gradient * gradient
    m1_o[...] = new_one
    m2_o[...] = new_two
    update = new_one / correct_one / (jnp.sqrt(new_two / correct_two) + epsilon)
    master = w_v[...]
    stepped = master - learn_rate * (update + weight_decay * master)
    w_v[...] = stepped
    ss[...] = stepped.astype(BF)
    ys = [remote(ss, sr.at[0], y_s.at[0], y_r.at[0], (after, me))]
    if nb > 2:
        ys.append(remote(ss, sr.at[1], y_s.at[1], y_r.at[1], (before, me)))
    for y in ys:
        y.start()

    for zz in range(nz):
        a_x_in(zz).wait_recv()
        core_a(zz, c).start()
    group = 1
    while (group * 4 * R) % 128:
        group += 1
    rows = group * 4 * R
    tokens = tok2[0:T, :]
    upstream = cot2[0:T, :]
    total = jnp.zeros((T, H), F32)
    for first in range(0, nz, group):
        for zz in range(first, first + group):
            core_a(zz, 1 - c).wait_recv()
            core_b(zz, 1 - c).wait_recv()
        block = wfull[first : first + group].reshape(rows, H)
        span = slice(first * 4 * R, first * 4 * R + rows)
        total += jnp.dot(tokens[:, span], block, preferred_element_type=F32)
        ig_o[:, span] = (
            lax.dot_general(upstream, block, (((1,), (1,)), ((), ())), preferred_element_type=F32) * factor
        ).astype(BF)
    key_o[...] = (total * factor).astype(BF)

    left = gos[0, 0].astype(F32)
    self_ = gos[0, 1].astype(F32)
    right = gos[0, 2].astype(F32)
    for y in ys:
        y.wait_recv()
    from_before = sr[0].astype(F32)
    from_after = sr[1].astype(F32) if nb > 2 else from_before
    weight = jnp.full((R, H), left + self_ + right, F32)
    avg_o[...] = (left * from_before + self_ * w_v[...] + right * from_after) / weight

    ex_c.wait_send()
    ex_t.wait_send()
    b_x.wait_send()
    for y in ys:
        y.wait_send()
    red_bx.wait_send()
    for zz in range(nz):
        a_x(zz).wait_send()
        core_a(zz, c).wait_send()
        core_b(zz, c).wait_send()
        red_x(zz).wait_send()
        for d in (0, 1):
            from_here = (zz <= z) & (z < nz - 1) if d == 0 else (zz >= z) & (z > 0)

            @pl.when(from_here)
            def _():
                a_z(d, zz).wait_send()
                b_z(d, zz).wait_send()

            @pl.when((zz > z) if d == 0 else (zz < z))
            def _():
                red_za(d, zz).wait_send()
                red_zb(d, zz).wait_send()


def local(nz, nb, tokens, cotangent, weights, moment_one, moment_two, gossip):
    _, T, D = tokens.shape
    _, R, H = weights.shape
    n = nz * 4
    factor = 1.0 / math.sqrt(D)
    cut = 16 * max(1, round(R / 16 * 5 / 9))
    high = R - cut
    dma = pltpu.SemaphoreType.DMA
    vmem = pl.BlockSpec(memory_space=pltpu.VMEM)
    hbm = pl.BlockSpec(memory_space=pl.ANY)
    outs = pl.pallas_call(
        functools.partial(kernel, nz, nb, cut, factor),
        out_shape=(
            jax.ShapeDtypeStruct((T, H), BF),
            jax.ShapeDtypeStruct((T, D), BF),
            jax.ShapeDtypeStruct((R, H), F32),
            jax.ShapeDtypeStruct((R, H), F32),
            jax.ShapeDtypeStruct((R, H), F32),
        ),
        in_specs=[hbm] * 5 + [pl.BlockSpec(memory_space=pltpu.SMEM)],
        out_specs=(vmem,) * 5,
        scratch_shapes=[
            pltpu.VMEM((R, H), F32),
            pltpu.VMEM((R, H), F32),
            pltpu.VMEM((R, H), F32),
            pltpu.VMEM((2 * T, D), BF),
            pltpu.VMEM((2 * T, H), BF),
            pltpu.VMEM((nz, 2, 2, R, H), BF),
            pltpu.VMEM((D, H), F32),
            pltpu.VMEM((nz, cut, H), BF),
            pltpu.VMEM((nz, cut, H), BF),
            pltpu.VMEM((2, nz, cut, H), BF),
            pltpu.VMEM((2, nz, cut, H), BF),
            pltpu.VMEM((2, nz, 2, high, H), BF),
            pltpu.VMEM((2, nz, 2, high, H), BF),
            pltpu.VMEM((high, H), BF),
            pltpu.VMEM((high, H), BF),
            pltpu.VMEM((R, H), BF),
            pltpu.VMEM((2, R, H), BF),
            dma((5,)),
            dma((2,)), dma((2,)),
            dma((2, nz)), dma((nz,)),
            dma((nz,)), dma((nz,)),
            dma, dma,
            dma((2, nz)), dma((nz,)),
            dma((nz,)), dma((nz,)),
            dma((nz,)), dma((nz,)),
            dma((nz,)), dma((nz,)),
            dma((2, nz)), dma((2, nz)),
            dma((2, nz)), dma((2, nz)),
            dma, dma,
            dma((2,)), dma((2,)),
        ],
        compiler_params=pltpu.CompilerParams(
            collective_id=0, has_side_effects=True, vmem_limit_bytes=48 * 1024 * 1024
        ),
        name="step",
    )(tokens[0], cotangent[0], weights[0], moment_one[0], moment_two[0], gossip)
    return tuple(out[None] for out in outs)


def solution(mesh):
    wide = P("blk", "fsdp", None)
    nz = mesh.shape["fsdp"] // 4
    return jax.shard_map(
        functools.partial(local, nz, mesh.shape["blk"]),
        mesh=mesh,
        in_specs=(wide,) * 5 + (P("blk", None),),
        out_specs=(wide,) * 5,
        check_vma=False,
    )
```

```python
import functools
import math

import jax
import jax.numpy as jnp
from jax import lax
from jax.experimental import pallas as pl
from jax.experimental.pallas import tpu as pltpu
from jax.sharding import PartitionSpec as P

beta_one = 0.9
beta_two = 0.95
learn_rate = 0.05
weight_decay = 0.1
epsilon = 1e-08
correct_one = 1.0 - beta_one**5
correct_two = 1.0 - beta_two**5

BF = jnp.bfloat16
F32 = jnp.float32


def kernel(
    nz, nb, cut, factor,
    tok_h, cot_h, w_h, m1_h, m2_h, gos_h,
    key_o, ig_o, avg_o, m1_o, m2_o,
    gos, w_v, m1_v, m2_v, tok2, cot2, wfull, part,
    xs_a, xr_a, zs_a, zr_a, zs_b, zr_b, xs_b, xr_b, ss, sr,
    load_sem, ce_s, ce_r, az_s, az_r, ax_s, ax_r, bx_s, bx_r, bz_s, bz_r,
    ca_s, ca_r, cb_s, cb_r, rax_s, rax_r, rza_s, rza_r, rzb_s, rzb_r, rbx_s, rbx_r, y_s, y_r,
):
    T, D = tok_h.shape
    R, H = w_h.shape
    me = lax.axis_index("fsdp")
    rep = lax.axis_index("blk")
    z = me // 4
    x = (me // 2) % 2
    c = me % 2
    low, high = cut, R - cut

    def dev(zz, xx, cc):
        return (rep, zz * 4 + xx * 2 + cc)

    def remote(src, dst, s, r, device):
        return pltpu.make_async_remote_copy(
            src_ref=src, dst_ref=dst, send_sem=s, recv_sem=r,
            device_id=device, device_id_type=pl.DeviceIdType.MESH,
        )

    loads = [
        pltpu.make_async_copy(w_h, w_v, load_sem.at[0]),
        pltpu.make_async_copy(cot_h, cot2.at[0:T], load_sem.at[1]),
        pltpu.make_async_copy(tok_h, tok2.at[0:T], load_sem.at[2]),
        pltpu.make_async_copy(m1_h, m1_v, load_sem.at[3]),
        pltpu.make_async_copy(m2_h, m2_v, load_sem.at[4]),
        pltpu.make_async_copy(gos_h, gos, load_sem.at[5]),
    ]
    for load in loads:
        load.start()

    barrier = pltpu.get_barrier_semaphore()

    def greet(device):
        pl.semaphore_signal(barrier, inc=1, device_id=device, device_id_type=pl.DeviceIdType.MESH)

    after = lax.rem(rep + 1, nb)
    before = lax.rem(rep + nb - 1, nb)
    x_dev = dev(z, 1 - x, c)
    c_dev = dev(z, x, 1 - c)
    greet(x_dev)
    greet(c_dev)
    greet((after, me))
    if nb > 2:
        greet((before, me))

    @pl.when(z > 0)
    def _():
        greet(dev(z - 1, x, c))

    @pl.when(z < nz - 1)
    def _():
        greet(dev(z + 1, x, c))

    loads[0].wait()
    wfull[z, x, c] = w_v[...].astype(BF)
    pl.semaphore_wait(barrier, (3 if nb > 2 else 2) + jnp.minimum(z, 1) + jnp.minimum(nz - 1 - z, 1) + (1 if nb > 1 else 0))

    ex_c = remote(cot_h, cot2.at[T : 2 * T], ce_s.at[0], ce_r.at[0], c_dev)
    ex_t = remote(tok_h, tok2.at[T : 2 * T], ce_s.at[1], ce_r.at[1], c_dev)
    ex_c.start()
    ex_t.start()

    def a_z(d, zz):
        ref = wfull.at[zz, x, c, 0:low]
        return remote(ref, ref, az_s.at[d, zz], az_r.at[zz], dev(z + 1 - 2 * d, x, c))

    def a_x(zz):
        ref = wfull.at[zz, x, c, 0:low]
        return remote(ref, ref, ax_s.at[zz], ax_r.at[zz], x_dev)

    def a_x_in(zz):
        ref = wfull.at[zz, 1 - x, c, 0:low]
        return remote(ref, ref, ax_s.at[zz], ax_r.at[zz], x_dev)

    own_b = wfull.at[z, x, c, low:R]
    b_x = remote(own_b, own_b, bx_s, bx_r, x_dev)

    def b_z(d, zz):
        ref = wfull.at[zz, :, c, low:R]
        return remote(ref, ref, bz_s.at[d, zz], bz_r.at[zz], dev(z + 1 - 2 * d, x, c))

    def core_a(zz, cc):
        ref = wfull.at[zz, :, cc, 0:low]
        return remote(ref, ref, ca_s.at[zz], ca_r.at[zz], c_dev)

    def core_b(zz, cc):
        ref = wfull.at[zz, :, cc, low:R]
        return remote(ref, ref, cb_s.at[zz], cb_r.at[zz], c_dev)

    b_x.start()

    @pl.when(z < nz - 1)
    def _():
        a_z(0, z).start()

    @pl.when(z > 0)
    def _():
        a_z(1, z).start()

    a_x(z).start()

    def gather_pair():
        b_x.wait_recv()

        @pl.when(z < nz - 1)
        def _():
            b_z(0, z).start()

        @pl.when(z > 0)
        def _():
            b_z(1, z).start()

        core_b(z, c).start()

    def gather_hop(k):
        for d in (0, 1):
            zz = z - k if d == 0 else z + k

            @pl.when((zz >= 0) & (zz < nz))
            def _():
                further = (z < nz - 1) if d == 0 else (z > 0)
                a_z(d, zz).wait_recv()

                @pl.when(further)
                def _():
                    a_z(d, zz).start()

                a_x(zz).start()
                b_z(d, zz).wait_recv()

                @pl.when(further)
                def _():
                    b_z(d, zz).start()

                core_b(zz, c).start()

    gather_pair()

    loads[1].wait()
    loads[2].wait()
    ex_c.wait_recv()
    ex_t.wait_recv()
    wide = math.gcd(D, 384)

    def partial(j, carry):
        at = pl.multiple_of(j * wide, wide)
        part[pl.ds(at, wide), :] = lax.dot_general(
            tok2[:, pl.ds(at, wide)], cot2[...], (((0,), (0,)), ((), ())), preferred_element_type=F32
        )
        return carry

    lax.fori_loop(0, D // wide, partial, 0)

    def mine(zz, xx, start, size):
        at = pl.multiple_of((zz * 4 + xx * 2 + c) * R + start, 16)
        return part[pl.ds(at, size), :]

    up_first = jnp.where(z >= nz // 2, 1, 0)

    def red_x(zz):
        return remote(xs_a.at[zz], xr_a.at[zz], rax_s.at[zz], rax_r.at[zz], x_dev)

    def send_a(k, carry):
        zz = (1 - up_first) * (nz - 1 - k) + up_first * k
        xs_a[zz] = mine(zz, 1 - x, 0, low).astype(BF)
        red_x(zz).start()
        return carry

    lax.fori_loop(0, nz, send_a, 0)

    def red_za(d, zz):
        return remote(zs_a.at[d, zz], zr_a.at[d, zz], rza_s.at[d, zz], rza_r.at[d, zz], dev(z + 1 - 2 * d, x, c))

    def red_zb(d, zz):
        return remote(zs_b.at[d, zz], zr_b.at[d, zz], rzb_s.at[d, zz], rzb_r.at[d, zz], dev(z + 1 - 2 * d, x, c))

    def chain(d, body):
        count = (1 - d) * (nz - 1 - z) + d * z
        fed = (1 - d) * z + d * (nz - 1 - z) > 0

        def step(k, carry):
            body((1 - d) * (nz - 1 - k) + d * k, fed)
            return carry

        lax.fori_loop(0, count, step, 0)

    def chain_a(d):
        def body(zz, fed):
            red_x(zz).wait_recv()
            base = mine(zz, x, 0, low) + xr_a[zz].astype(F32)

            @pl.when(fed)
            def _():
                red_za(d, zz).wait_recv()
                zs_a[d, zz] = (base + zr_a[d, zz].astype(F32)).astype(BF)

            @pl.when(jnp.logical_not(fed))
            def _():
                zs_a[d, zz] = base.astype(BF)

            red_za(d, zz).start()

        chain(d, body)

    def chain_b(d):
        def body(zz, fed):
            @pl.when(fed)
            def _():
                red_zb(d, zz).wait_recv()
                for xx in (0, 1):
                    zs_b[d, zz, xx] = (mine(zz, xx, low, high) + zr_b[d, zz, xx].astype(F32)).astype(BF)

            @pl.when(jnp.logical_not(fed))
            def _():
                for xx in (0, 1):
                    zs_b[d, zz, xx] = mine(zz, xx, low, high).astype(BF)

            red_zb(d, zz).start()

        chain(d, body)

    at_end = (z == 0) | (z == nz - 1)

    @pl.when(at_end)
    def _():
        chain_b(up_first)
        gather_hop(1)
        chain_a(up_first)
        for k in range(2, nz):
            gather_hop(k)

    @pl.when(jnp.logical_not(at_end))
    def _():
        gather_hop(1)
        chain_b(up_first)
        if nz > 2:
            gather_hop(2)
        chain_b(1 - up_first)
        chain_a(up_first)
        for k in range(3, nz):
            gather_hop(k)
        chain_a(1 - up_first)

    def own_at(xx, start):
        return pl.ds(pl.multiple_of((z * 4 + xx * 2 + c) * R + start, 16), low if start == 0 else high)

    for d in (0, 1):
        @pl.when((z > 0) if d == 0 else (z < nz - 1))
        def _():
            red_zb(d, z).wait_recv()
            for xx in (0, 1):
                part[own_at(xx, low), :] += zr_b[d, z, xx].astype(F32)

    red_bx = remote(xs_b, xr_b, rbx_s, rbx_r, x_dev)
    xs_b[...] = mine(z, 1 - x, low, high).astype(BF)
    red_bx.start()
    red_x(z).wait_recv()
    part[own_at(x, 0), :] += xr_a[z].astype(F32)
    for d in (0, 1):
        @pl.when((z > 0) if d == 0 else (z < nz - 1))
        def _():
            red_za(d, z).wait_recv()
            part[own_at(x, 0), :] += zr_a[d, z].astype(F32)

    loads[3].wait()
    loads[4].wait()

    def to(peer, side, index, start, size):
        return remote(
            ss.at[start : start + size], sr.at[side, start : start + size],
            y_s.at[side, index], y_r.at[side, index], (peer, me),
        )

    ys = []

    def optimize(index, start, size):
        span = slice(start, start + size)
        gradient = part[own_at(x, start), :] * factor
        new_one = beta_one * m1_v[span] + (1.0 - beta_one) * gradient
        new_two = beta_two * m2_v[span] + (1.0 - beta_two) * gradient * gradient
        m1_o[span] = new_one
        m2_o[span] = new_two
        update = new_one / correct_one / (jnp.sqrt(new_two / correct_two) + epsilon)
        master = w_v[span]
        stepped = master - learn_rate * (update + weight_decay * master)
        w_v[span] = stepped
        ss[span] = stepped.astype(BF)
        pair = [to(after, 0, index, start, size)]
        if nb > 2:
            pair.append(to(before, 1, index, start, size))
        for y in pair:
            y.start()
        ys.extend(pair)

    optimize(0, 0, low)
    red_bx.wait_recv()
    part[own_at(x, low), :] += xr_b[...].astype(F32)
    optimize(1, low, high)

    for zz in range(nz):
        a_x_in(zz).wait_recv()
        core_a(zz, c).start()
    group = 1
    while (group * 4 * R) % 128:
        group += 1
    rows = group * 4 * R
    tokens = tok2[0:T, :]
    upstream = cot2[0:T, :]
    total = jnp.zeros((T, H), F32)
    for first in range(0, nz, group):
        for zz in range(first, first + group):
            core_a(zz, 1 - c).wait_recv()
            core_b(zz, 1 - c).wait_recv()
        block = wfull[first : first + group].reshape(rows, H)
        span = slice(first * 4 * R, first * 4 * R + rows)
        total += jnp.dot(tokens[:, span], block, preferred_element_type=F32)
        ig_o[:, span] = (
            lax.dot_general(upstream, block, (((1,), (1,)), ((), ())), preferred_element_type=F32) * factor
        ).astype(BF)
    key_o[...] = (total * factor).astype(BF)

    loads[5].wait()
    left = gos[0, 0].astype(F32)
    self_ = gos[0, 1].astype(F32)
    right = gos[0, 2].astype(F32)
    for y in ys:
        y.wait_recv()
    from_before = sr[0].astype(F32)
    from_after = sr[1].astype(F32) if nb > 2 else from_before
    weight = jnp.full((R, H), left + self_ + right, F32)
    avg_o[...] = (left * from_before + self_ * w_v[...] + right * from_after) / weight

    ex_c.wait_send()
    ex_t.wait_send()
    b_x.wait_send()
    for y in ys:
        y.wait_send()
    red_bx.wait_send()
    for zz in range(nz):
        a_x(zz).wait_send()
        core_a(zz, c).wait_send()
        core_b(zz, c).wait_send()
        red_x(zz).wait_send()
        for d in (0, 1):
            from_here = (zz <= z) & (z < nz - 1) if d == 0 else (zz >= z) & (z > 0)

            @pl.when(from_here)
            def _():
                a_z(d, zz).wait_send()
                b_z(d, zz).wait_send()

            @pl.when((zz > z) if d == 0 else (zz < z))
            def _():
                red_za(d, zz).wait_send()
                red_zb(d, zz).wait_send()


def put_out(*refs):
    ins, outs, sem = refs[:5], refs[5:10], refs[10]
    copies = [pltpu.make_async_copy(a, b, sem.at[i]) for i, (a, b) in enumerate(zip(ins, outs))]
    for copy in copies:
        copy.start()
    for copy in copies:
        copy.wait()


def local(nz, nb, tokens, cotangent, weights, moment_one, moment_two, gossip):
    _, T, D = tokens.shape
    _, R, H = weights.shape
    n = nz * 4
    factor = 1.0 / math.sqrt(D)
    cut = 16 * max(1, round(R / 16 * 5 / 9))
    high = R - cut
    dma = pltpu.SemaphoreType.DMA
    vmem = pl.BlockSpec(memory_space=pltpu.VMEM)
    hbm = pl.BlockSpec(memory_space=pl.ANY)
    outs = pl.pallas_call(
        functools.partial(kernel, nz, nb, cut, factor),
        out_shape=(
            jax.ShapeDtypeStruct((T, H), BF),
            jax.ShapeDtypeStruct((T, D), BF),
            jax.ShapeDtypeStruct((R, H), F32),
            jax.ShapeDtypeStruct((R, H), F32),
            jax.ShapeDtypeStruct((R, H), F32),
        ),
        in_specs=[hbm] * 6,
        out_specs=(vmem,) * 5,
        scratch_shapes=[
            pltpu.SMEM(gossip.shape, gossip.dtype),
            pltpu.VMEM((R, H), F32),
            pltpu.VMEM((R, H), F32),
            pltpu.VMEM((R, H), F32),
            pltpu.VMEM((2 * T, D), BF),
            pltpu.VMEM((2 * T, H), BF),
            pltpu.VMEM((nz, 2, 2, R, H), BF),
            pltpu.VMEM((D, H), F32),
            pltpu.VMEM((nz, cut, H), BF),
            pltpu.VMEM((nz, cut, H), BF),
            pltpu.VMEM((2, nz, cut, H), BF),
            pltpu.VMEM((2, nz, cut, H), BF),
            pltpu.VMEM((2, nz, 2, high, H), BF),
            pltpu.VMEM((2, nz, 2, high, H), BF),
            pltpu.VMEM((high, H), BF),
            pltpu.VMEM((high, H), BF),
            pltpu.VMEM((R, H), BF),
            pltpu.VMEM((2, R, H), BF),
            dma((6,)),
            dma((2,)), dma((2,)),
            dma((2, nz)), dma((nz,)),
            dma((nz,)), dma((nz,)),
            dma, dma,
            dma((2, nz)), dma((nz,)),
            dma((nz,)), dma((nz,)),
            dma((nz,)), dma((nz,)),
            dma((nz,)), dma((nz,)),
            dma((2, nz)), dma((2, nz)),
            dma((2, nz)), dma((2, nz)),
            dma, dma,
            dma((2, 2)), dma((2, 2)),
        ],
        compiler_params=pltpu.CompilerParams(
            collective_id=0, has_side_effects=True
        ),
        name="step",
    )(tokens[0], cotangent[0], weights[0], moment_one[0], moment_two[0], gossip)
    outs = pl.pallas_call(
        put_out,
        out_shape=tuple(jax.ShapeDtypeStruct(out.shape, out.dtype) for out in outs),
        in_specs=[vmem] * 5,
        out_specs=(hbm,) * 5,
        scratch_shapes=[dma((5,))],
        name="put_out",
    )(*outs)
    return tuple(out[None] for out in outs)


def solution(mesh):
    wide = P("blk", "fsdp", None)
    nz = mesh.shape["fsdp"] // 4
    return jax.shard_map(
        functools.partial(local, nz, mesh.shape["blk"]),
        mesh=mesh,
        in_specs=(wide,) * 5 + (P("blk", None),),
        out_specs=(wide,) * 5,
        check_vma=False,
    )
```

```python
import functools
import math

import jax
import jax.numpy as jnp
from jax import lax
from jax.experimental import pallas as pl
from jax.experimental.pallas import tpu as pltpu
from jax.sharding import PartitionSpec as P

beta_one = 0.9
beta_two = 0.95
learn_rate = 0.05
weight_decay = 0.1
epsilon = 1e-08
correct_one = 1.0 - beta_one**5
correct_two = 1.0 - beta_two**5

BF = jnp.bfloat16
F32 = jnp.float32


def kernel(
    nz, nb, keep, cut, factor,
    tok_h, cot_h, w_h, m1_h, m2_h, gos_h,
    key_o, ig_o, avg_o, m1_o, m2_o,
    gos, w_v, m1_v, m2_v, tok2, cot2, wfull, part,
    xs_a, xr_a, zs_a, zr_a, zs_b, zr_b, xs_b, xr_b, ss, sr,
    load_sem, ce_s, ce_r, az_s, az_r, ax_s, ax_r, bx_s, bx_r, bz_s, bz_r,
    ca_s, ca_r, cb_s, cb_r, rax_s, rax_r, rza_s, rza_r, rzb_s, rzb_r, rbx_s, rbx_r, y_s, y_r,
):
    T, D = tok_h.shape
    R, H = w_h.shape
    me = lax.axis_index("fsdp")
    rep = lax.axis_index("blk")
    z = me // 4
    x = (me // 2) % 2
    c = me % 2
    low, high = cut, R - cut

    def dev(zz, xx, cc):
        return (rep, zz * 4 + xx * 2 + cc)

    def remote(src, dst, s, r, device):
        return pltpu.make_async_remote_copy(
            src_ref=src, dst_ref=dst, send_sem=s, recv_sem=r,
            device_id=device, device_id_type=pl.DeviceIdType.MESH,
        )

    loads = [
        pltpu.make_async_copy(w_h, w_v, load_sem.at[0]),
        pltpu.make_async_copy(cot_h, cot2.at[0:T], load_sem.at[1]),
        pltpu.make_async_copy(tok_h, tok2.at[0:T], load_sem.at[2]),
        pltpu.make_async_copy(m1_h, m1_v, load_sem.at[3]),
        pltpu.make_async_copy(m2_h, m2_v, load_sem.at[4]),
        pltpu.make_async_copy(gos_h, gos, load_sem.at[5]),
    ]
    for load in loads:
        load.start()

    barrier = pltpu.get_barrier_semaphore()

    def greet(device):
        pl.semaphore_signal(barrier, inc=1, device_id=device, device_id_type=pl.DeviceIdType.MESH)

    after = lax.rem(rep + 1, nb)
    before = lax.rem(rep + nb - 1, nb)
    x_dev = dev(z, 1 - x, c)
    c_dev = dev(z, x, 1 - c)
    greet(x_dev)
    greet(c_dev)
    greet((after, me))
    if nb > 2:
        greet((before, me))

    def greet_column(k, carry):
        greet(dev(lax.rem(z + k, nz), x, c))
        return carry

    lax.fori_loop(1, nz, greet_column, 0)
    loads[0].wait()
    wfull[z, x, c] = w_v[...].astype(BF)
    pl.semaphore_wait(barrier, (4 if nb > 2 else 3) + nz - 1)

    ex_c = remote(cot_h, cot2.at[T : 2 * T], ce_s.at[0], ce_r.at[0], c_dev)
    ex_t = remote(tok_h, tok2.at[T : 2 * T], ce_s.at[1], ce_r.at[1], c_dev)
    ex_c.start()
    ex_t.start()

    def a_z(d, zz):
        ref = wfull.at[zz, x, c, 0:keep]
        return remote(ref, ref, az_s.at[d, zz], az_r.at[zz], dev(z + 1 - 2 * d, x, c))

    def a_x(zz):
        ref = wfull.at[zz, x, c, 0:keep]
        return remote(ref, ref, ax_s.at[zz], ax_r.at[zz], x_dev)

    def a_x_in(zz):
        ref = wfull.at[zz, 1 - x, c, 0:keep]
        return remote(ref, ref, ax_s.at[zz], ax_r.at[zz], x_dev)

    own_b = wfull.at[z, x, c, keep:R]
    b_x = remote(own_b, own_b, bx_s, bx_r, x_dev)

    def b_z(d, zz):
        ref = wfull.at[zz, :, c, keep:R]
        return remote(ref, ref, bz_s.at[d, zz], bz_r.at[zz], dev(z + 1 - 2 * d, x, c))

    def core_a(zz, cc):
        ref = wfull.at[zz, :, cc, 0:keep]
        return remote(ref, ref, ca_s.at[zz], ca_r.at[zz], c_dev)

    def core_b(zz, cc):
        ref = wfull.at[zz, :, cc, keep:R]
        return remote(ref, ref, cb_s.at[zz], cb_r.at[zz], c_dev)

    b_x.start()

    @pl.when(z < nz - 1)
    def _():
        a_z(0, z).start()

    @pl.when(z > 0)
    def _():
        a_z(1, z).start()

    a_x(z).start()

    def gather_pair():
        b_x.wait_recv()

        @pl.when(z < nz - 1)
        def _():
            b_z(0, z).start()

        @pl.when(z > 0)
        def _():
            b_z(1, z).start()

        core_b(z, c).start()

    def gather_hop(k):
        for d in (0, 1):
            zz = z - k if d == 0 else z + k

            @pl.when((zz >= 0) & (zz < nz))
            def _():
                further = (z < nz - 1) if d == 0 else (z > 0)
                a_z(d, zz).wait_recv()

                @pl.when(further)
                def _():
                    a_z(d, zz).start()

                a_x(zz).start()
                b_z(d, zz).wait_recv()

                @pl.when(further)
                def _():
                    b_z(d, zz).start()

                core_b(zz, c).start()

    gather_pair()

    loads[1].wait()
    loads[2].wait()
    ex_c.wait_recv()
    ex_t.wait_recv()
    group = 1
    while (group * 4 * R) % 128:
        group += 1
    rows = group * 4 * R
    wide = math.gcd(rows, 384)

    def mine(zz, xx, start, size):
        at = pl.multiple_of((zz * 4 + xx * 2 + c) * R + start, 16)
        return part[pl.ds(at, size), :]

    def red_x(zz):
        return remote(xs_a.at[zz], xr_a.at[zz], rax_s.at[zz], rax_r.at[zz], x_dev)

    def red_za(zz, source):
        return remote(zs_a.at[zz], zr_a.at[source], rza_s.at[zz], rza_r.at[source], dev(zz, x, c))

    def red_zb(zz, source):
        return remote(zs_b.at[zz], zr_b.at[source], rzb_s.at[zz], rzb_r.at[source], dev(zz, x, c))

    def first_sends(zz):
        @pl.when(zz != z)
        def _():
            for xx in (0, 1):
                zs_b[zz, xx] = mine(zz, xx, low, high).astype(BF)
            red_zb(zz, z).start()

        xs_a[zz] = mine(zz, 1 - x, 0, low).astype(BF)
        red_x(zz).start()

    def second_sends(zz):
        @pl.when(zz != z)
        def _():
            red_x(zz).wait_recv()
            zs_a[zz] = (mine(zz, x, 0, low) + xr_a[zz].astype(F32)).astype(BF)
            red_za(zz, z).start()

    def ordered(step, k):
        slot = lax.rem(z // group + 1 + k // group, nz // group)
        step(slot * group + k % group)

    for k in range(0, nz, group):
        base = lax.rem(z // group + 1 + k // group, nz // group) * rows
        for j in range(rows // wide):
            at = pl.multiple_of(base + j * wide, wide)
            part[pl.ds(at, wide), :] = lax.dot_general(
                tok2[:, pl.ds(at, wide)], cot2[...], (((0,), (0,)), ((), ())), preferred_element_type=F32
            )
        for i in range(group):
            ordered(first_sends, k + i)

    gather_hop(1)
    for k in range(nz):
        ordered(second_sends, k)
    for k in range(2, nz):
        gather_hop(k)

    def own_at(xx, start):
        return pl.ds(pl.multiple_of((z * 4 + xx * 2 + c) * R + start, 16), low if start == 0 else high)

    def sum_b(k, carry):
        source = lax.rem(z + k, nz)
        red_zb(z, source).wait_recv()
        for xx in (0, 1):
            part[own_at(xx, low), :] += zr_b[source, xx].astype(F32)
        return carry

    lax.fori_loop(1, nz, sum_b, 0)
    red_bx = remote(xs_b, xr_b, rbx_s, rbx_r, x_dev)
    xs_b[...] = mine(z, 1 - x, low, high).astype(BF)
    red_bx.start()
    red_x(z).wait_recv()
    part[own_at(x, 0), :] += xr_a[z].astype(F32)

    def sum_a(k, carry):
        source = lax.rem(z + k, nz)
        red_za(z, source).wait_recv()
        part[own_at(x, 0), :] += zr_a[source].astype(F32)
        return carry

    lax.fori_loop(1, nz, sum_a, 0)
    loads[3].wait()
    loads[4].wait()

    def to(peer, side, index, start, size):
        return remote(
            ss.at[start : start + size], sr.at[side, start : start + size],
            y_s.at[side, index], y_r.at[side, index], (peer, me),
        )

    ys = []

    def optimize(index, start, size):
        span = slice(start, start + size)
        gradient = part[own_at(x, start), :] * factor
        new_one = beta_one * m1_v[span] + (1.0 - beta_one) * gradient
        new_two = beta_two * m2_v[span] + (1.0 - beta_two) * gradient * gradient
        m1_o[span] = new_one
        m2_o[span] = new_two
        update = new_one / correct_one / (jnp.sqrt(new_two / correct_two) + epsilon)
        master = w_v[span]
        stepped = master - learn_rate * (update + weight_decay * master)
        w_v[span] = stepped
        ss[span] = stepped.astype(BF)
        pair = [to(after, 0, index, start, size)]
        if nb > 2:
            pair.append(to(before, 1, index, start, size))
        for y in pair:
            y.start()
        ys.extend(pair)

    optimize(0, 0, low)
    slots = [lax.rem(z // group + g, nz // group) for g in range(nz // group)]

    def pass_on(slot):
        for i in range(group):
            zz = slot * group + i
            a_x_in(zz).wait_recv()
            core_a(zz, c).start()

    pass_on(slots[0])
    red_bx.wait_recv()
    part[own_at(x, low), :] += xr_b[...].astype(F32)
    optimize(1, low, high)

    upstream = cot2[0:T, :]
    total = jnp.zeros((T, H), F32)
    for g, slot in enumerate(slots):
        if g > 0:
            pass_on(slot)
        for i in range(group):
            core_a(slot * group + i, 1 - c).wait_recv()
            core_b(slot * group + i, 1 - c).wait_recv()
        block = wfull[pl.ds(slot * group, group)].reshape(rows, H)
        span = pl.ds(pl.multiple_of(slot * rows, rows), rows)
        total += jnp.dot(tok2[0:T, span], block, preferred_element_type=F32)
        ig_o[:, span] = (
            lax.dot_general(upstream, block, (((1,), (1,)), ((), ())), preferred_element_type=F32) * factor
        ).astype(BF)
    key_o[...] = (total * factor).astype(BF)

    loads[5].wait()
    left = gos[0, 0].astype(F32)
    self_ = gos[0, 1].astype(F32)
    right = gos[0, 2].astype(F32)
    for y in ys:
        y.wait_recv()
    from_before = sr[0].astype(F32)
    from_after = sr[1].astype(F32) if nb > 2 else from_before
    weight = jnp.full((R, H), left + self_ + right, F32)
    avg_o[...] = (left * from_before + self_ * w_v[...] + right * from_after) / weight

    ex_c.wait_send()
    ex_t.wait_send()
    b_x.wait_send()
    for y in ys:
        y.wait_send()
    red_bx.wait_send()
    for zz in range(nz):
        a_x(zz).wait_send()
        core_a(zz, c).wait_send()
        core_b(zz, c).wait_send()
        red_x(zz).wait_send()
        for d in (0, 1):
            from_here = (zz <= z) & (z < nz - 1) if d == 0 else (zz >= z) & (z > 0)

            @pl.when(from_here)
            def _():
                a_z(d, zz).wait_send()
                b_z(d, zz).wait_send()

        @pl.when(zz != z)
        def _():
            red_za(zz, z).wait_send()
            red_zb(zz, z).wait_send()


def put_out(*refs):
    ins, outs, sem = refs[:5], refs[5:10], refs[10]
    copies = [pltpu.make_async_copy(a, b, sem.at[i]) for i, (a, b) in enumerate(zip(ins, outs))]
    for copy in copies:
        copy.start()
    for copy in copies:
        copy.wait()


def local(nz, nb, tokens, cotangent, weights, moment_one, moment_two, gossip):
    _, T, D = tokens.shape
    _, R, H = weights.shape
    n = nz * 4
    factor = 1.0 / math.sqrt(D)
    keep = 16 * max(1, min(R // 16 - 1, round(R / 16 * 7 / 9)))
    cut = 16 * max(1, min(R // 16 - 1, round(R / 16 * 8 / 9)))
    high = R - cut
    dma = pltpu.SemaphoreType.DMA
    vmem = pl.BlockSpec(memory_space=pltpu.VMEM)
    hbm = pl.BlockSpec(memory_space=pl.ANY)
    outs = pl.pallas_call(
        functools.partial(kernel, nz, nb, keep, cut, factor),
        out_shape=(
            jax.ShapeDtypeStruct((T, H), BF),
            jax.ShapeDtypeStruct((T, D), BF),
            jax.ShapeDtypeStruct((R, H), F32),
            jax.ShapeDtypeStruct((R, H), F32),
            jax.ShapeDtypeStruct((R, H), F32),
        ),
        in_specs=[hbm] * 6,
        out_specs=(vmem,) * 5,
        scratch_shapes=[
            pltpu.SMEM(gossip.shape, gossip.dtype),
            pltpu.VMEM((R, H), F32),
            pltpu.VMEM((R, H), F32),
            pltpu.VMEM((R, H), F32),
            pltpu.VMEM((2 * T, D), BF),
            pltpu.VMEM((2 * T, H), BF),
            pltpu.VMEM((nz, 2, 2, R, H), BF),
            pltpu.VMEM((D, H), F32),
            pltpu.VMEM((nz, cut, H), BF),
            pltpu.VMEM((nz, cut, H), BF),
            pltpu.VMEM((nz, cut, H), BF),
            pltpu.VMEM((nz, cut, H), BF),
            pltpu.VMEM((nz, 2, high, H), BF),
            pltpu.VMEM((nz, 2, high, H), BF),
            pltpu.VMEM((high, H), BF),
            pltpu.VMEM((high, H), BF),
            pltpu.VMEM((R, H), BF),
            pltpu.VMEM((2, R, H), BF),
            dma((6,)),
            dma((2,)), dma((2,)),
            dma((2, nz)), dma((nz,)),
            dma((nz,)), dma((nz,)),
            dma, dma,
            dma((2, nz)), dma((nz,)),
            dma((nz,)), dma((nz,)),
            dma((nz,)), dma((nz,)),
            dma((nz,)), dma((nz,)),
            dma((nz,)), dma((nz,)),
            dma((nz,)), dma((nz,)),
            dma, dma,
            dma((2, 2)), dma((2, 2)),
        ],
        compiler_params=pltpu.CompilerParams(
            collective_id=0, has_side_effects=True, vmem_limit_bytes=48 * 1024 * 1024
        ),
        name="step",
    )(*(pltpu.with_memory_space_constraint(v, pltpu.HBM) for v in (tokens[0], cotangent[0], weights[0], moment_one[0], moment_two[0], gossip)))
    outs = pl.pallas_call(
        put_out,
        out_shape=tuple(jax.ShapeDtypeStruct(out.shape, out.dtype) for out in outs),
        in_specs=[vmem] * 5,
        out_specs=(hbm,) * 5,
        scratch_shapes=[dma((5,))],
        compiler_params=pltpu.CompilerParams(vmem_limit_bytes=16 * 1024 * 1024),
        name="put_out",
    )(*outs)
    return tuple(out[None] for out in outs)


def solution(mesh):
    wide = P("blk", "fsdp", None)
    nz = mesh.shape["fsdp"] // 4
    return jax.shard_map(
        functools.partial(local, nz, mesh.shape["blk"]),
        mesh=mesh,
        in_specs=(wide,) * 5 + (P("blk", None),),
        out_specs=(wide,) * 5,
        check_vma=False,
    )
```

```python
import functools
import math

import jax
import jax.numpy as jnp
from jax import lax
from jax.experimental import pallas as pl
from jax.experimental.pallas import tpu as pltpu
from jax.sharding import PartitionSpec as P

beta_one = 0.9
beta_two = 0.95
learn_rate = 0.05
weight_decay = 0.1
epsilon = 1e-08
correct_one = 1.0 - beta_one**5
correct_two = 1.0 - beta_two**5

BF = jnp.bfloat16
F32 = jnp.float32


def kernel(
    nz, nb, cut, factor,
    tok_h, cot_h, w_h, m1_h, m2_h, gos_h,
    key_o, ig_o, avg_o, m1_o, m2_o,
    gos, w_v, m1_v, m2_v, tok2, cot2, wfull, part,
    xs_a, xr_a, zs_a, zr_a, zs_b, zr_b, xs_b, xr_b, ss, sr,
    load_sem, ce_s, ce_r, az_s, az_r, ax_s, ax_r, bx_s, bx_r, bz_s, bz_r,
    ca_s, ca_r, cb_s, cb_r, rax_s, rax_r, rza_s, rza_r, rzb_s, rzb_r, rbx_s, rbx_r, y_s, y_r,
):
    T, D = tok_h.shape
    R, H = w_h.shape
    me = lax.axis_index("fsdp")
    rep = lax.axis_index("blk")
    z = me // 4
    x = (me // 2) % 2
    c = me % 2
    low, high = cut, R - cut

    def dev(zz, xx, cc):
        return (rep, zz * 4 + xx * 2 + cc)

    def remote(src, dst, s, r, device):
        return pltpu.make_async_remote_copy(
            src_ref=src, dst_ref=dst, send_sem=s, recv_sem=r,
            device_id=device, device_id_type=pl.DeviceIdType.MESH,
        )

    loads = [
        pltpu.make_async_copy(w_h, w_v, load_sem.at[0]),
        pltpu.make_async_copy(cot_h, cot2.at[0:T], load_sem.at[1]),
        pltpu.make_async_copy(tok_h, tok2.at[0:T], load_sem.at[2]),
        pltpu.make_async_copy(m1_h, m1_v, load_sem.at[3]),
        pltpu.make_async_copy(m2_h, m2_v, load_sem.at[4]),
        pltpu.make_async_copy(gos_h, gos, load_sem.at[5]),
    ]
    for load in loads:
        load.start()

    barrier = pltpu.get_barrier_semaphore()

    def greet(device):
        pl.semaphore_signal(barrier, inc=1, device_id=device, device_id_type=pl.DeviceIdType.MESH)

    after = lax.rem(rep + 1, nb)
    before = lax.rem(rep + nb - 1, nb)
    x_dev = dev(z, 1 - x, c)
    c_dev = dev(z, x, 1 - c)
    greet(x_dev)
    greet(c_dev)
    greet((after, me))
    if nb > 2:
        greet((before, me))

    @pl.when(z > 0)
    def _():
        greet(dev(z - 1, x, c))

    @pl.when(z < nz - 1)
    def _():
        greet(dev(z + 1, x, c))

    loads[0].wait()
    wfull[z, x, c] = w_v[...].astype(BF)
    pl.semaphore_wait(barrier, (3 if nb > 2 else 2) + jnp.minimum(z, 1) + jnp.minimum(nz - 1 - z, 1) + (1 if nb > 1 else 0))

    ex_c = remote(cot_h, cot2.at[T : 2 * T], ce_s.at[0], ce_r.at[0], c_dev)
    ex_t = remote(tok_h, tok2.at[T : 2 * T], ce_s.at[1], ce_r.at[1], c_dev)
    ex_c.start()
    ex_t.start()

    def a_z(d, zz):
        ref = wfull.at[zz, x, c, 0:low]
        return remote(ref, ref, az_s.at[d, zz], az_r.at[zz], dev(z + 1 - 2 * d, x, c))

    def a_x(zz):
        ref = wfull.at[zz, x, c, 0:low]
        return remote(ref, ref, ax_s.at[zz], ax_r.at[zz], x_dev)

    def a_x_in(zz):
        ref = wfull.at[zz, 1 - x, c, 0:low]
        return remote(ref, ref, ax_s.at[zz], ax_r.at[zz], x_dev)

    own_b = wfull.at[z, x, c, low:R]
    b_x = remote(own_b, own_b, bx_s, bx_r, x_dev)

    def b_z(d, zz):
        ref = wfull.at[zz, :, c, low:R]
        return remote(ref, ref, bz_s.at[d, zz], bz_r.at[zz], dev(z + 1 - 2 * d, x, c))

    def core_a(zz, cc):
        ref = wfull.at[zz, :, cc, 0:low]
        return remote(ref, ref, ca_s.at[zz], ca_r.at[zz], c_dev)

    def core_b(zz, cc):
        ref = wfull.at[zz, :, cc, low:R]
        return remote(ref, ref, cb_s.at[zz], cb_r.at[zz], c_dev)

    b_x.start()

    @pl.when(z < nz - 1)
    def _():
        a_z(0, z).start()

    @pl.when(z > 0)
    def _():
        a_z(1, z).start()

    a_x(z).start()

    def gather_pair():
        b_x.wait_recv()

        @pl.when(z < nz - 1)
        def _():
            b_z(0, z).start()

        @pl.when(z > 0)
        def _():
            b_z(1, z).start()

        core_b(z, c).start()

    def gather_hop(k):
        for d in (0, 1):
            zz = z - k if d == 0 else z + k

            @pl.when((zz >= 0) & (zz < nz))
            def _():
                further = (z < nz - 1) if d == 0 else (z > 0)
                a_z(d, zz).wait_recv()

                @pl.when(further)
                def _():
                    a_z(d, zz).start()

                a_x(zz).start()
                b_z(d, zz).wait_recv()

                @pl.when(further)
                def _():
                    b_z(d, zz).start()

                core_b(zz, c).start()

    gather_pair()

    loads[1].wait()
    loads[2].wait()
    ex_c.wait_recv()
    ex_t.wait_recv()
    wide = math.gcd(D, 384)

    def partial(j, carry):
        at = pl.multiple_of(j * wide, wide)
        part[pl.ds(at, wide), :] = lax.dot_general(
            tok2[:, pl.ds(at, wide)], cot2[...], (((0,), (0,)), ((), ())), preferred_element_type=F32
        )
        return carry

    lax.fori_loop(0, D // wide, partial, 0)

    def mine(zz, xx, start, size):
        at = pl.multiple_of((zz * 4 + xx * 2 + c) * R + start, 16)
        return part[pl.ds(at, size), :]

    up_first = jnp.where(z >= nz // 2, 1, 0)

    def red_x(zz):
        return remote(xs_a.at[zz], xr_a.at[zz], rax_s.at[zz], rax_r.at[zz], x_dev)

    def send_a(k, carry):
        zz = (1 - up_first) * (nz - 1 - k) + up_first * k
        xs_a[zz] = mine(zz, 1 - x, 0, low).astype(BF)
        red_x(zz).start()
        return carry

    lax.fori_loop(0, nz, send_a, 0)

    def red_za(d, zz):
        return remote(zs_a.at[d, zz], zr_a.at[d, zz], rza_s.at[d, zz], rza_r.at[d, zz], dev(z + 1 - 2 * d, x, c))

    def red_zb(d, zz):
        return remote(zs_b.at[d, zz], zr_b.at[d, zz], rzb_s.at[d, zz], rzb_r.at[d, zz], dev(z + 1 - 2 * d, x, c))

    def chain(d, body):
        count = (1 - d) * (nz - 1 - z) + d * z
        fed = (1 - d) * z + d * (nz - 1 - z) > 0

        def step(k, carry):
            body((1 - d) * (nz - 1 - k) + d * k, fed)
            return carry

        lax.fori_loop(0, count, step, 0)

    def chain_a(d):
        def body(zz, fed):
            red_x(zz).wait_recv()
            base = mine(zz, x, 0, low) + xr_a[zz].astype(F32)

            @pl.when(fed)
            def _():
                red_za(d, zz).wait_recv()
                zs_a[d, zz] = (base + zr_a[d, zz].astype(F32)).astype(BF)

            @pl.when(jnp.logical_not(fed))
            def _():
                zs_a[d, zz] = base.astype(BF)

            red_za(d, zz).start()

        chain(d, body)

    def chain_b(d):
        def body(zz, fed):
            @pl.when(fed)
            def _():
                red_zb(d, zz).wait_recv()
                for xx in (0, 1):
                    zs_b[d, zz, xx] = (mine(zz, xx, low, high) + zr_b[d, zz, xx].astype(F32)).astype(BF)

            @pl.when(jnp.logical_not(fed))
            def _():
                for xx in (0, 1):
                    zs_b[d, zz, xx] = mine(zz, xx, low, high).astype(BF)

            red_zb(d, zz).start()

        chain(d, body)

    at_end = (z == 0) | (z == nz - 1)

    @pl.when(at_end)
    def _():
        chain_b(up_first)
        gather_hop(1)
        chain_a(up_first)
        for k in range(2, nz):
            gather_hop(k)

    @pl.when(jnp.logical_not(at_end))
    def _():
        gather_hop(1)
        chain_b(up_first)
        if nz > 2:
            gather_hop(2)
        chain_b(1 - up_first)
        chain_a(up_first)
        for k in range(3, nz):
            gather_hop(k)
        chain_a(1 - up_first)

    def own_at(xx, start):
        return pl.ds(pl.multiple_of((z * 4 + xx * 2 + c) * R + start, 16), low if start == 0 else high)

    for d in (0, 1):
        @pl.when((z > 0) if d == 0 else (z < nz - 1))
        def _():
            red_zb(d, z).wait_recv()
            for xx in (0, 1):
                part[own_at(xx, low), :] += zr_b[d, z, xx].astype(F32)

    red_bx = remote(xs_b, xr_b, rbx_s, rbx_r, x_dev)
    xs_b[...] = mine(z, 1 - x, low, high).astype(BF)
    red_bx.start()
    red_x(z).wait_recv()
    part[own_at(x, 0), :] += xr_a[z].astype(F32)
    for d in (0, 1):
        @pl.when((z > 0) if d == 0 else (z < nz - 1))
        def _():
            red_za(d, z).wait_recv()
            part[own_at(x, 0), :] += zr_a[d, z].astype(F32)

    loads[3].wait()
    loads[4].wait()

    def to(peer, side, index, start, size):
        return remote(
            ss.at[start : start + size], sr.at[side, start : start + size],
            y_s.at[side, index], y_r.at[side, index], (peer, me),
        )

    ys = []

    def optimize(index, start, size):
        span = slice(start, start + size)
        gradient = part[own_at(x, start), :] * factor
        new_one = beta_one * m1_v[span] + (1.0 - beta_one) * gradient
        new_two = beta_two * m2_v[span] + (1.0 - beta_two) * gradient * gradient
        m1_o[span] = new_one
        m2_o[span] = new_two
        update = new_one / correct_one / (jnp.sqrt(new_two / correct_two) + epsilon)
        master = w_v[span]
        stepped = master - learn_rate * (update + weight_decay * master)
        w_v[span] = stepped
        ss[span] = stepped.astype(BF)
        pair = [to(after, 0, index, start, size)]
        if nb > 2:
            pair.append(to(before, 1, index, start, size))
        for y in pair:
            y.start()
        ys.extend(pair)

    optimize(0, 0, low)
    red_bx.wait_recv()
    part[own_at(x, low), :] += xr_b[...].astype(F32)
    optimize(1, low, high)

    for zz in range(nz):
        a_x_in(zz).wait_recv()
        core_a(zz, c).start()
    group = 1
    while (group * 4 * R) % 128:
        group += 1
    rows = group * 4 * R
    tokens = tok2[0:T, :]
    upstream = cot2[0:T, :]
    total = jnp.zeros((T, H), F32)
    for first in range(0, nz, group):
        for zz in range(first, first + group):
            core_a(zz, 1 - c).wait_recv()
            core_b(zz, 1 - c).wait_recv()
        block = wfull[first : first + group].reshape(rows, H)
        span = slice(first * 4 * R, first * 4 * R + rows)
        total += jnp.dot(tokens[:, span], block, preferred_element_type=F32)
        ig_o[:, span] = (
            lax.dot_general(upstream, block, (((1,), (1,)), ((), ())), preferred_element_type=F32) * factor
        ).astype(BF)
    key_o[...] = (total * factor).astype(BF)

    loads[5].wait()
    left = gos[0, 0].astype(F32)
    self_ = gos[0, 1].astype(F32)
    right = gos[0, 2].astype(F32)
    for y in ys:
        y.wait_recv()
    from_before = sr[0].astype(F32)
    from_after = sr[1].astype(F32) if nb > 2 else from_before
    weight = jnp.full((R, H), left + self_ + right, F32)
    avg_o[...] = (left * from_before + self_ * w_v[...] + right * from_after) / weight

    ex_c.wait_send()
    ex_t.wait_send()
    b_x.wait_send()
    for y in ys:
        y.wait_send()
    red_bx.wait_send()
    for zz in range(nz):
        a_x(zz).wait_send()
        core_a(zz, c).wait_send()
        core_b(zz, c).wait_send()
        red_x(zz).wait_send()
        for d in (0, 1):
            from_here = (zz <= z) & (z < nz - 1) if d == 0 else (zz >= z) & (z > 0)

            @pl.when(from_here)
            def _():
                a_z(d, zz).wait_send()
                b_z(d, zz).wait_send()

            @pl.when((zz > z) if d == 0 else (zz < z))
            def _():
                red_za(d, zz).wait_send()
                red_zb(d, zz).wait_send()


def put_out(*refs):
    ins, outs, sem = refs[:5], refs[5:10], refs[10]
    copies = [pltpu.make_async_copy(a, b, sem.at[i]) for i, (a, b) in enumerate(zip(ins, outs))]
    for copy in copies:
        copy.start()
    for copy in copies:
        copy.wait()


def local(nz, nb, tokens, cotangent, weights, moment_one, moment_two, gossip):
    _, T, D = tokens.shape
    _, R, H = weights.shape
    n = nz * 4
    factor = 1.0 / math.sqrt(D)
    cut = 16 * max(1, round(R / 16 * 7 / 9))
    high = R - cut
    dma = pltpu.SemaphoreType.DMA
    vmem = pl.BlockSpec(memory_space=pltpu.VMEM)
    hbm = pl.BlockSpec(memory_space=pl.ANY)
    outs = pl.pallas_call(
        functools.partial(kernel, nz, nb, cut, factor),
        out_shape=(
            jax.ShapeDtypeStruct((T, H), BF),
            jax.ShapeDtypeStruct((T, D), BF),
            jax.ShapeDtypeStruct((R, H), F32),
            jax.ShapeDtypeStruct((R, H), F32),
            jax.ShapeDtypeStruct((R, H), F32),
        ),
        in_specs=[hbm] * 6,
        out_specs=(vmem,) * 5,
        scratch_shapes=[
            pltpu.SMEM(gossip.shape, gossip.dtype),
            pltpu.VMEM((R, H), F32),
            pltpu.VMEM((R, H), F32),
            pltpu.VMEM((R, H), F32),
            pltpu.VMEM((2 * T, D), BF),
            pltpu.VMEM((2 * T, H), BF),
            pltpu.VMEM((nz, 2, 2, R, H), BF),
            pltpu.VMEM((D, H), F32),
            pltpu.VMEM((nz, cut, H), BF),
            pltpu.VMEM((nz, cut, H), BF),
            pltpu.VMEM((2, nz, cut, H), BF),
            pltpu.VMEM((2, nz, cut, H), BF),
            pltpu.VMEM((2, nz, 2, high, H), BF),
            pltpu.VMEM((2, nz, 2, high, H), BF),
            pltpu.VMEM((high, H), BF),
            pltpu.VMEM((high, H), BF),
            pltpu.VMEM((R, H), BF),
            pltpu.VMEM((2, R, H), BF),
            dma((6,)),
            dma((2,)), dma((2,)),
            dma((2, nz)), dma((nz,)),
            dma((nz,)), dma((nz,)),
            dma, dma,
            dma((2, nz)), dma((nz,)),
            dma((nz,)), dma((nz,)),
            dma((nz,)), dma((nz,)),
            dma((nz,)), dma((nz,)),
            dma((2, nz)), dma((2, nz)),
            dma((2, nz)), dma((2, nz)),
            dma, dma,
            dma((2, 2)), dma((2, 2)),
        ],
        compiler_params=pltpu.CompilerParams(
            collective_id=0, has_side_effects=True, vmem_limit_bytes=48 * 1024 * 1024
        ),
        name="step",
    )(*(pltpu.with_memory_space_constraint(v, pltpu.HBM) for v in (tokens[0], cotangent[0], weights[0], moment_one[0], moment_two[0], gossip)))
    outs = pl.pallas_call(
        put_out,
        out_shape=tuple(jax.ShapeDtypeStruct(out.shape, out.dtype) for out in outs),
        in_specs=[vmem] * 5,
        out_specs=(hbm,) * 5,
        scratch_shapes=[dma((5,))],
        compiler_params=pltpu.CompilerParams(vmem_limit_bytes=16 * 1024 * 1024),
        name="put_out",
    )(*outs)
    return tuple(out[None] for out in outs)


def solution(mesh):
    wide = P("blk", "fsdp", None)
    nz = mesh.shape["fsdp"] // 4
    return jax.shard_map(
        functools.partial(local, nz, mesh.shape["blk"]),
        mesh=mesh,
        in_specs=(wide,) * 5 + (P("blk", None),),
        out_specs=(wide,) * 5,
        check_vma=False,
    )
```
